32 devices in a mesh: row: 8 (over z, core), col: 4 (over y, x).
Axes of the slice: x: 2, y: 2, z: 4, core: 2. Of those that a mesh axis runs over, the one named last changes fastest.
Arguments:
- labels_prior: float32 [16, 65536], P(None, ('row', 'col')), may hold values from 0.05 to 1
- tiles: bfloat16 [7168, 128, 128], P(('row', 'col')), may hold values from 0 to 1
- tile_rows: int32 [7168], P(('row', 'col')), may hold values from 0 to 63, as said below
- tile_cols: int32 [7168], P(('row', 'col')), may hold values from 0 to 127, as said below
- tile_count: int32 [32], P(('row', 'col')), may hold values from 28 to 224, as said below
Outputs:
- scores: float32 [16, 65536], P(None, ('row', 'col'))
The draws below stay inside these ranges and needn't reach their ends.
Inputs may be any that keep to these rules, and one draw needn't show every extreme that they name: `tile_rows`: block rows within a row group of 16 * 4 blocks; both ends occur. `tile_cols`: block columns within a column group of 16 * 8 blocks; both ends occur. `tile_count`: loads are skewed; some device uses all 224 slots.
All inputs are finite; a program needn't handle non-finite values.
Results may differ from the reference program's by a relative error of at most 0.0003.
Values may be sent and summed in bfloat16 or wider, within the bound.
A program may use at most 64 MiB of HBM per device.

```python
import math
import jax
import jax.numpy as jnp
from jax import lax

TILE = 128
LABELS = 16
BPP = 16
ITERS = 2
CAP = 224
NODES = 65536
N_ROW = 8
N_COL = 4


def draw_tile_rows(key, part):
    total = N_ROW * N_COL * CAP
    inner = jax.random.fold_in(key, 11)
    values = jax.random.randint(inner, (total,), 0, N_COL * BPP, dtype=jnp.int32)
    return values.at[0].set(0).at[total - 1].set(N_COL * BPP - 1)


def draw_tile_cols(key, part):
    total = N_ROW * N_COL * CAP
    inner = jax.random.fold_in(key, 12)
    values = jax.random.randint(inner, (total,), 0, N_ROW * BPP, dtype=jnp.int32)
    return values.at[1].set(N_ROW * BPP - 1).at[total - 2].set(0)


def draw_tile_count(key, part):
    devices = N_ROW * N_COL
    lowest = CAP // 8
    inner = jax.random.fold_in(key, 13)
    first = jax.random.randint(jax.random.fold_in(inner, 1), (devices,), 0, CAP - lowest + 1, dtype=jnp.int32)
    second = jax.random.randint(jax.random.fold_in(inner, 2), (devices,), 0, CAP - lowest + 1, dtype=jnp.int32)
    counts = lowest + jnp.minimum(first, second)
    busiest = jax.random.randint(jax.random.fold_in(inner, 3), (), 0, devices, dtype=jnp.int32)
    return jnp.where(jnp.arange(devices, dtype=jnp.int32) == busiest, CAP, counts).astype(jnp.int32)


def shard_levels(own_key, shape, split, least, top_value):
    def one(axis_at, blocks):
        steps = jax.random.uniform(jax.random.fold_in(jax.random.fold_in(own_key, 6), axis_at), (blocks,), jnp.float32, least / len(split), top_value / len(split))
        return jnp.repeat(jnp.exp(steps), shape[axis_at] // blocks).reshape((-1,) + (1,) * (len(shape) - axis_at - 1))

    gain = one(*split[0])
    for cut in split[1:]:
        gain = gain * one(*cut)
    return gain


def setup_inputs(seed: int = 0) -> dict:
    streams_of = jax.random.split(jax.random.key(seed), 6)
    labels_prior = jnp.clip(jnp.exp(math.log(1.0) - 2.9957323 * jax.random.uniform(streams_of[0], (LABELS, NODES), jnp.float32) ** shard_levels(streams_of[0], (LABELS, NODES), ((1, 32),), -0.2, 0.2)), 0.05, 1.0)
    tiles = jnp.clip(1.0 * jax.random.uniform(streams_of[1], (N_ROW * N_COL * CAP, TILE, TILE), jnp.float32) ** shard_levels(streams_of[1], (N_ROW * N_COL * CAP, TILE, TILE), ((0, 32),), -0.2, 0.2), 0.0, 1.0).astype(jnp.bfloat16)
    tile_rows = draw_tile_rows(jax.random.fold_in(streams_of[5], 71), 0)
    tile_cols = draw_tile_cols(jax.random.fold_in(streams_of[5], 71), 0)
    tile_count = draw_tile_count(jax.random.fold_in(streams_of[5], 71), 0)
    return dict(labels_prior=labels_prior, tiles=tiles, tile_rows=tile_rows, tile_cols=tile_cols, tile_count=tile_count)


spread_weight = 0.9


def reference(labels_prior, tiles, tile_rows, tile_cols, tile_count):
    devices = N_ROW * N_COL
    group_blocks = N_COL * BPP
    group_nodes = group_blocks * TILE
    tile_four = tiles.reshape(devices, CAP, TILE, TILE)
    rows_two = tile_rows.reshape(devices, CAP)
    cols_two = tile_cols.reshape(devices, CAP)
    slot_ids = jnp.arange(CAP, dtype=jnp.int32)
    block_ids = jnp.arange(group_blocks, dtype=jnp.int32)
    device_ids = jnp.arange(devices, dtype=jnp.int32)

    def hot_rows(device):
        valid = (slot_ids < tile_count[device]).astype(jnp.float32)
        return (rows_two[device][:, None] == block_ids[None, :]).astype(jnp.float32) * valid[:, None]

    def global_cols(device):
        column = device % N_COL
        local = cols_two[device]
        return ((local // BPP * N_COL + column) * BPP + local % BPP).astype(jnp.int32)

    def degree_step(total, device):
        rowsum = jnp.sum(tile_four[device].astype(jnp.float32), axis=2)
        part = jnp.einsum("sr,si->ri", hot_rows(device), rowsum, precision=lax.Precision.HIGHEST).reshape(-1)
        start = ((device // N_COL) * group_nodes).astype(jnp.int32)
        current = lax.dynamic_slice_in_dim(total, start, group_nodes, 0)
        return lax.dynamic_update_slice_in_dim(total, current + part, start, 0), None

    degree = lax.scan(degree_step, jnp.zeros((NODES,), jnp.float32), device_ids)[0] + 1.0

    scores = labels_prior
    for step in range(ITERS):
        blocks = scores.astype(jnp.bfloat16).reshape(LABELS, NODES // TILE, TILE)

        def add_device(total, device):
            picked = jnp.take(blocks, global_cols(device), axis=1)
            terms = jnp.einsum("lsj,sij->sli", picked.astype(jnp.float32), tile_four[device].astype(jnp.float32), precision=lax.Precision.HIGHEST)
            part = jnp.einsum("sr,sli->lri", hot_rows(device), terms, precision=lax.Precision.HIGHEST).reshape(LABELS, group_nodes)
            start = ((device // N_COL) * group_nodes).astype(jnp.int32)
            current = lax.dynamic_slice_in_dim(total, start, group_nodes, 1)
            return lax.dynamic_update_slice_in_dim(total, current + part, start, 1), None

        sums = lax.scan(add_device, jnp.zeros((LABELS, NODES), jnp.float32), device_ids)[0]
        scores = spread_weight * (sums + scores) / degree[None, :] + (1.0 - spread_weight) * labels_prior
    return scores
```

```python
import functools

import jax
import jax.numpy as jnp
from jax import lax
from jax.experimental import pallas as pl
from jax.experimental.pallas import tpu as pltpu
from jax.sharding import PartitionSpec as P

ITERS = 2
SPREAD = 0.9
LEVELS = 65535.0
CHUNKS = 2
LOADS = 8
UNROLL = 8


def plan(tile_rows, tile_cols, tile_count, group_blocks):
    slots = tile_rows.shape[0]
    ids = jnp.arange(slots, dtype=jnp.int32)
    row = jnp.where(ids < tile_count[0], tile_rows, group_blocks)
    key = row * slots + ids
    rank = jnp.sum((key[None, :] < key[:, None]).astype(jnp.int32), axis=1)
    hit = rank[:, None] == ids[None, :]
    order = jnp.sum(jnp.where(hit, ids[:, None], 0), axis=0)
    cols = jnp.sum(jnp.where(hit, tile_cols[:, None], 0), axis=0)
    here = jnp.sum(jnp.where(hit, row[:, None] + 1, 0), axis=0)
    before = jnp.sum(jnp.where(rank[:, None] + 1 == ids[None, :], row[:, None] + 1, 0), axis=0)
    keep = (here == before).astype(jnp.int32)
    group = jnp.arange(group_blocks, dtype=jnp.int32)
    stop = jnp.sum((row[:, None] <= group[None, :]).astype(jnp.int32), axis=0)
    start = jnp.sum((row[:, None] < group[None, :]).astype(jnp.int32), axis=0)
    used = (stop > start).astype(jnp.int32)
    last = jnp.maximum(stop - 1, 0)
    return order, cols, keep, last, used


def kernel(
    n_row, n_col,
    prior_ref, tiles_hbm, order_ref, cols_ref, keep_ref, last_ref, used_ref,
    out_ref,
    tiles_ref, ag0_ref, ag1_ref, run_ref, rows_ref, inv_ref, rows_in_ref, code_ref, code_in_ref,
    cur_ref, scale_ref,
    load_sem, ag_send, ag_recv, rs_send, rs_recv, row_send, row_recv,
):
    labels, piece = prior_ref.shape
    slots, tile, _ = tiles_ref.shape
    own = piece // tile
    part = own // CHUNKS
    gathered = (ag0_ref, ag1_ref)
    n_z = n_row // 2
    my_row = lax.axis_index("row")
    my_col = lax.axis_index("col")
    my_z = my_row // 2
    my_core = my_row % 2
    partner = my_z * 2 + (1 - my_core)

    def at(row, col):
        return {"row": row, "col": col}

    loads = []
    step = slots // LOADS
    for n in range(LOADS):
        window = pl.ds(n * step, step)
        loads.append(
            pltpu.make_async_copy(tiles_hbm.at[window], tiles_ref.at[window], load_sem.at[n])
        )
        loads[-1].start()

    barrier = pltpu.get_barrier_semaphore()
    z_to = [None] + [((my_z + d) % n_z) * 2 + my_core for d in range(1, n_z)]
    z_from = [None] + [((my_z + n_z - d) % n_z) * 2 + my_core for d in range(1, n_z)]
    c_to = [None] + [(my_col + d) % n_col for d in range(1, n_col)]
    c_from = [None] + [(my_col + n_col - d) % n_col for d in range(1, n_col)]
    for d in range(1, n_z):
        pl.semaphore_signal(barrier, inc=1, device_id=at(z_to[d], my_col))
    pl.semaphore_signal(barrier, inc=1, device_id=at(partner, my_col))
    for d in range(1, n_col):
        pl.semaphore_signal(barrier, inc=1, device_id=at(my_row, c_to[d]))

    def gather_copy(it, src_row, c, slot, to_row):
        window = pl.ds(src_row * own + c * part, part)
        return pltpu.make_async_remote_copy(
            src_ref=gathered[it].at[window],
            dst_ref=gathered[it].at[window],
            send_sem=ag_send.at[it, slot, c],
            recv_sem=ag_recv.at[it, slot, c],
            device_id=at(to_row, my_col),
        )

    def gather_start(it, c):
        copies = []
        for d in list(range(n_z - 1, 0, -1)):
            copies.append(gather_copy(it, my_row, c, d, z_to[d]))
        copies.append(gather_copy(it, my_row, c, n_z, partner))
        for copy in copies:
            copy.start()
        return copies

    def gather_finish(it):
        copies = []
        for c in range(CHUNKS):
            for d in range(1, n_z):
                gather_copy(it, z_from[d], c, d, z_to[d]).wait_recv()
                copy = gather_copy(it, z_from[d], c, n_z + d, partner)
                copy.start()
                copies.append(copy)
        for c in range(CHUNKS):
            for d in range(n_z):
                gather_copy(it, my_row, c, n_z + d, partner).wait_recv()
        return copies

    def lanes(b):
        return pl.ds(pl.multiple_of(b * tile, tile), tile)

    def round_prior(b, carry):
        value = prior_ref[:, lanes(b)]
        cur_ref[b] = value
        ag0_ref[my_row * own + b] = value.astype(jnp.bfloat16)
        return carry

    lax.fori_loop(0, own, round_prior, 0)
    pl.semaphore_wait(barrier, n_z + n_col - 1)
    sent = []
    for c in range(CHUNKS):
        sent += gather_start(0, c)

    def product(left, slot):
        return lax.dot_general(
            left, tiles_ref[slot], (((1,), (1,)), ((), ())), preferred_element_type=jnp.float32
        )

    for copy in loads:
        copy.wait()
    ones = jnp.ones((labels, tile), jnp.bfloat16)

    def sum_slot(k, total):
        total = total * keep_ref[k].astype(jnp.float32) + product(ones, order_ref[k])
        run_ref[k] = total
        return total

    lax.fori_loop(0, slots, sum_slot, jnp.zeros((labels, tile), jnp.float32), unroll=UNROLL)

    def pick_rows(r, carry):
        value = run_ref[last_ref[r]] * used_ref[r].astype(jnp.float32)
        rows_ref[pl.ds(r, 1), :] = value[0:1, :]
        return carry

    lax.fori_loop(0, n_col * own, pick_rows, 0, unroll=8)

    def row_copy(d):
        return pltpu.make_async_remote_copy(
            src_ref=rows_ref.at[pl.ds(pl.multiple_of(c_to[d] * own, own), own)],
            dst_ref=rows_in_ref.at[d],
            send_sem=row_send.at[d],
            recv_sem=row_recv.at[d],
            device_id=at(my_row, c_to[d]),
        )

    for d in range(1, n_col):
        copy = row_copy(d)
        copy.start()
        sent.append(copy)
    whole = rows_ref[...]
    inv_ref[...] = jnp.where(whole > 0.0, LEVELS / jnp.where(whole > 0.0, whole, 1.0), 0.0)

    sent += gather_finish(0)

    def code_copy(it, d, c):
        return pltpu.make_async_remote_copy(
            src_ref=code_ref.at[it, pl.ds(c_to[d] * own + c * part, part)],
            dst_ref=code_in_ref.at[it, d, pl.ds(c * part, part)],
            send_sem=rs_send.at[it, d, c],
            recv_sem=rs_recv.at[it, d, c],
            device_id=at(my_row, c_to[d]),
        )

    for it in range(ITERS):

        def add_slot(k, total):
            total = total * keep_ref[k].astype(jnp.float32) + product(
                gathered[it][cols_ref[k]], order_ref[k]
            )
            run_ref[k] = total
            return total

        lax.fori_loop(0, slots, add_slot, jnp.zeros((labels, tile), jnp.float32), unroll=UNROLL)

        for c in range(CHUNKS):
            for d in range(1, n_col):

                def encode(b, carry):
                    r = c_to[d] * own + c * part + b
                    value = run_ref[last_ref[r]] * used_ref[r].astype(jnp.float32)
                    level = jnp.minimum(value * inv_ref[pl.ds(r, 1), :] + 0.5, LEVELS)
                    code_ref[it, r] = (level.astype(jnp.int32) - 32768).astype(jnp.int16)
                    return carry

                lax.fori_loop(0, part, encode, 0, unroll=True)
                copy = code_copy(it, d, c)
                copy.start()
                sent.append(copy)

        if it == 0:
            degree = 1.0 + rows_ref[pl.ds(pl.multiple_of(my_col * own, own), own), :]
            for d in range(1, n_col):
                row_copy(d).wait_recv()
                degree = degree + rows_in_ref[d]
            scale_ref[...] = SPREAD / degree

        for c in range(CHUNKS):
            for d in range(1, n_col):
                code_copy(it, d, c).wait_recv()

            def update(n, carry):
                b = c * part + n
                r = my_col * own + b
                total = cur_ref[b] + run_ref[last_ref[r]] * used_ref[r].astype(jnp.float32)
                for d in range(1, n_col):
                    level = code_in_ref[it, d, b].astype(jnp.int32).astype(jnp.float32) + 32768.0
                    total = total + level * (rows_in_ref[d, pl.ds(b, 1), :] * (1.0 / LEVELS))
                value = total * scale_ref[pl.ds(b, 1), :] + (1.0 - SPREAD) * prior_ref[:, lanes(b)]
                if it + 1 < ITERS:
                    cur_ref[b] = value
                    gathered[it + 1][my_row * own + b] = value.astype(jnp.bfloat16)
                else:
                    out_ref[:, lanes(b)] = value
                return carry

            lax.fori_loop(0, part, update, 0, unroll=True)
            if it + 1 < ITERS:
                sent += gather_start(it + 1, c)
        if it + 1 < ITERS:
            sent += gather_finish(it + 1)

    for copy in sent:
        copy.wait_send()


def local(n_row, n_col, labels_prior, tiles, tile_rows, tile_cols, tile_count):
    labels, piece = labels_prior.shape
    slots, tile, _ = tiles.shape
    own = piece // tile
    n_z = n_row // 2
    group = n_col * own
    smem = pl.BlockSpec(memory_space=pltpu.SMEM)
    vmem = pl.BlockSpec(memory_space=pltpu.VMEM)
    return pl.pallas_call(
        functools.partial(kernel, n_row, n_col),
        out_shape=jax.ShapeDtypeStruct((labels, piece), jnp.float32),
        in_specs=[vmem, pl.BlockSpec(memory_space=pl.ANY)] + [smem] * 5,
        out_specs=vmem,
        scratch_shapes=[
            pltpu.VMEM((slots, tile, tile), jnp.bfloat16),
            pltpu.VMEM((n_row * own, labels, tile), jnp.bfloat16),
            pltpu.VMEM((n_row * own, labels, tile), jnp.bfloat16),
            pltpu.VMEM((slots, labels, tile), jnp.float32),
            pltpu.VMEM((group, tile), jnp.float32),
            pltpu.VMEM((group, tile), jnp.float32),
            pltpu.VMEM((n_col, own, tile), jnp.float32),
            pltpu.VMEM((ITERS, group, labels, tile), jnp.int16),
            pltpu.VMEM((ITERS, n_col, own, labels, tile), jnp.int16),
            pltpu.VMEM((own, labels, tile), jnp.float32),
            pltpu.VMEM((own, tile), jnp.float32),
            pltpu.SemaphoreType.DMA((LOADS,)),
            pltpu.SemaphoreType.DMA((ITERS, 2 * n_z, CHUNKS)),
            pltpu.SemaphoreType.DMA((ITERS, 2 * n_z, CHUNKS)),
            pltpu.SemaphoreType.DMA((ITERS, n_col, CHUNKS)),
            pltpu.SemaphoreType.DMA((ITERS, n_col, CHUNKS)),
            pltpu.SemaphoreType.DMA((n_col,)),
            pltpu.SemaphoreType.DMA((n_col,)),
        ],
        compiler_params=pltpu.CompilerParams(
            collective_id=0, has_side_effects=True, vmem_limit_bytes=56 * 1024 * 1024
        ),
    )(labels_prior, tiles, *plan(tile_rows, tile_cols, tile_count, group))


def solution(mesh):
    n_row, n_col = mesh.shape["row"], mesh.shape["col"]
    in_specs = (
        P(None, ("row", "col")),
        P(("row", "col"), None, None),
        P(("row", "col")),
        P(("row", "col")),
        P(("row", "col")),
    )
    return jax.shard_map(
        functools.partial(local, n_row, n_col),
        mesh=mesh,
        in_specs=in_specs,
        out_specs=P(None, ("row", "col")),
        check_vma=False,
    )
```

```python
import functools

import jax
import jax.numpy as jnp
from jax import lax
from jax.experimental import pallas as pl
from jax.experimental.pallas import tpu as pltpu
from jax.sharding import PartitionSpec as P

ITERS = 2
SPREAD = 0.9
LEVELS = 65535.0
CHUNKS = 2
LOADS = 7
UNROLL = 28


def plan(rows, cols, count, table_ref, group_blocks):
    slots = rows.shape[1]
    lane = lax.broadcasted_iota(jnp.int32, (slots, slots), 1)
    down = lax.broadcasted_iota(jnp.int32, (slots, slots), 0)
    row = jnp.where(lane[0:1] < count, rows, group_blocks)
    key = row * slots + lane[0:1]
    same = lane == down

    def stand(x):
        return jnp.sum(jnp.where(same, x, 0), axis=1, keepdims=True)

    key_down, row_down, col_down = stand(key), stand(row), stand(cols)
    rank = jnp.sum((key < key_down).astype(jnp.int32), axis=1, keepdims=True)
    hit = rank == lane

    def lie(cond, x):
        return jnp.sum(jnp.where(cond, x, 0), axis=0, keepdims=True)

    here = lie(hit, row_down + 1)
    before = lie(rank + 1 == lane, row_down + 1)
    table_ref[0:1, 0:slots] = lie(hit, down)
    table_ref[1:2, 0:slots] = lie(hit, col_down)
    table_ref[2:3, 0:slots] = (here == before).astype(jnp.int32)
    group = lax.broadcasted_iota(jnp.int32, (slots, group_blocks), 1)
    stop = jnp.sum((row_down <= group).astype(jnp.int32), axis=0, keepdims=True)
    start = jnp.sum((row_down < group).astype(jnp.int32), axis=0, keepdims=True)
    table_ref[3:4, 0:group_blocks] = jnp.maximum(stop - 1, 0)
    table_ref[4:5, 0:group_blocks] = (stop > start).astype(jnp.int32)
    block = lax.broadcasted_iota(jnp.int32, (group_blocks, slots), 0)
    return (block == row).astype(jnp.float32)


def kernel(
    n_row, n_col,
    prior_ref, tiles_hbm, slot_rows_ref, slot_cols_ref, count_ref,
    out_ref,
    tiles_ref, ag0_ref, ag1_ref, run_ref, rows_ref, inv_ref, rows_in_ref, code_ref, code_in_ref,
    cur_ref, scale_ref, table_ref, plan_ref, slot_sum_ref,
    load_sem, plan_sem, ag_send, ag_recv, rs_send, rs_recv, row_send, row_recv,
):
    labels, piece = prior_ref.shape
    slots, tile, _ = tiles_ref.shape
    own = piece // tile
    part = own // CHUNKS
    gathered = (ag0_ref, ag1_ref)
    n_z = n_row // 2
    my_row = lax.axis_index("row")
    my_col = lax.axis_index("col")
    my_z = my_row // 2
    my_core = my_row % 2
    partner = my_z * 2 + (1 - my_core)

    def at(row, col):
        return {"row": row, "col": col}

    loads = []
    step = slots // LOADS
    for n in range(LOADS):
        window = pl.ds(n * step, step)
        loads.append(
            pltpu.make_async_copy(tiles_hbm.at[window], tiles_ref.at[window], load_sem.at[n])
        )
        loads[-1].start()

    barrier = pltpu.get_barrier_semaphore()
    z_to = [None] + [((my_z + d) % n_z) * 2 + my_core for d in range(1, n_z)]
    z_from = [None] + [((my_z + n_z - d) % n_z) * 2 + my_core for d in range(1, n_z)]
    c_to = [None] + [(my_col + d) % n_col for d in range(1, n_col)]
    c_from = [None] + [(my_col + n_col - d) % n_col for d in range(1, n_col)]
    for d in range(1, n_z):
        pl.semaphore_signal(barrier, inc=1, device_id=at(z_to[d], my_col))
    pl.semaphore_signal(barrier, inc=1, device_id=at(partner, my_col))
    for d in range(1, n_col):
        pl.semaphore_signal(barrier, inc=1, device_id=at(my_row, c_to[d]))

    def gather_copy(it, src_row, c, slot, to_row):
        window = pl.ds(src_row * own + c * part, part)
        return pltpu.make_async_remote_copy(
            src_ref=gathered[it].at[window],
            dst_ref=gathered[it].at[window],
            send_sem=ag_send.at[it, slot, c],
            recv_sem=ag_recv.at[it, slot, c],
            device_id=at(to_row, my_col),
        )

    def gather_start(it, c):
        copies = []
        for d in list(range(n_z - 1, 0, -1)):
            copies.append(gather_copy(it, my_row, c, d, z_to[d]))
        copies.append(gather_copy(it, my_row, c, n_z, partner))
        for copy in copies:
            copy.start()
        return copies

    def gather_finish(it):
        copies = []
        for c in range(CHUNKS):
            for d in range(1, n_z):
                gather_copy(it, z_from[d], c, d, z_to[d]).wait_recv()
                copy = gather_copy(it, z_from[d], c, n_z + d, partner)
                copy.start()
                copies.append(copy)
        for c in range(CHUNKS):
            for d in range(n_z):
                gather_copy(it, my_row, c, n_z + d, partner).wait_recv()
        return copies

    def lanes(b):
        return pl.ds(pl.multiple_of(b * tile, tile), tile)

    def round_prior(b, carry):
        value = prior_ref[:, lanes(b)]
        cur_ref[b] = value
        ag0_ref[my_row * own + b] = value.astype(jnp.bfloat16)
        return carry

    lax.fori_loop(0, own, round_prior, 0)
    pl.semaphore_wait(barrier, n_z + n_col - 1)
    sent = []
    for c in range(CHUNKS):
        sent += gather_start(0, c)

    def product(left, right):
        return lax.dot_general(
            left, right, (((1,), (1,)), ((), ())), preferred_element_type=jnp.float32
        )

    hot = plan(slot_rows_ref[...], slot_cols_ref[...], count_ref[0], table_ref, n_col * own)
    plan_copy = pltpu.make_async_copy(table_ref, plan_ref, plan_sem)
    plan_copy.start()

    def pair(lefts, slot_pair):
        blank = jnp.zeros_like(lefts[0])
        left = jnp.concatenate(
            [
                jnp.concatenate([lefts[0], blank], axis=1),
                jnp.concatenate([blank, lefts[1]], axis=1),
            ],
            axis=0,
        )
        both = product(left, jnp.concatenate([tiles_ref[n] for n in slot_pair], axis=1))
        return both[:labels], both[labels:]

    ones = jnp.ones((labels, tile), jnp.bfloat16)
    for n, copy in enumerate(loads):
        copy.wait()

        def sum_pair(m, carry):
            k = n * step + 2 * m
            for i, value in enumerate(pair((ones, ones), (k, k + 1))):
                slot_sum_ref[pl.ds(k + i, 1), :] = value[0:1]
            return carry

        lax.fori_loop(0, step // 2, sum_pair, 0, unroll=True)
    rows_ref[...] = jnp.dot(
        hot, slot_sum_ref[...], precision=lax.Precision.HIGHEST, preferred_element_type=jnp.float32
    )

    def row_copy(d):
        return pltpu.make_async_remote_copy(
            src_ref=rows_ref.at[pl.ds(pl.multiple_of(c_to[d] * own, own), own)],
            dst_ref=rows_in_ref.at[d],
            send_sem=row_send.at[d],
            recv_sem=row_recv.at[d],
            device_id=at(my_row, c_to[d]),
        )

    for d in range(1, n_col):
        copy = row_copy(d)
        copy.start()
        sent.append(copy)
    whole = rows_ref[...]
    inv_ref[...] = jnp.where(whole > 0.0, LEVELS / jnp.where(whole > 0.0, whole, 1.0), 0.0)

    plan_copy.wait()
    sent += gather_finish(0)

    def code_copy(it, d, c):
        return pltpu.make_async_remote_copy(
            src_ref=code_ref.at[it, pl.ds(c_to[d] * own + c * part, part)],
            dst_ref=code_in_ref.at[it, d, pl.ds(c * part, part)],
            send_sem=rs_send.at[it, d, c],
            recv_sem=rs_recv.at[it, d, c],
            device_id=at(my_row, c_to[d]),
        )

    for it in range(ITERS):

        def add_pair(m, total):
            ks = (2 * m, 2 * m + 1)
            terms = pair(
                [gathered[it][plan_ref[1, k]] for k in ks], [plan_ref[0, k] for k in ks]
            )
            for k, term in zip(ks, terms):
                total = total * plan_ref[2, k].astype(jnp.float32) + term
                run_ref[k] = total
            return total

        lax.fori_loop(
            0, slots // 2, add_pair, jnp.zeros((labels, tile), jnp.float32), unroll=UNROLL
        )

        for c in range(CHUNKS):
            for d in range(1, n_col):

                def encode(b, carry):
                    r = c_to[d] * own + c * part + b
                    value = run_ref[plan_ref[3, r]] * plan_ref[4, r].astype(jnp.float32)
                    level = jnp.minimum(value * inv_ref[pl.ds(r, 1), :] + 0.5, LEVELS)
                    code_ref[it, r] = (level.astype(jnp.int32) - 32768).astype(jnp.int16)
                    return carry

                lax.fori_loop(0, part, encode, 0, unroll=True)
                copy = code_copy(it, d, c)
                copy.start()
                sent.append(copy)

        if it == 0:
            degree = 1.0 + rows_ref[pl.ds(pl.multiple_of(my_col * own, own), own), :]
            for d in range(1, n_col):
                row_copy(d).wait_recv()
                degree = degree + rows_in_ref[d]
            scale_ref[...] = SPREAD / degree

        for c in range(CHUNKS):
            for d in range(1, n_col):
                code_copy(it, d, c).wait_recv()

            def update(n, carry):
                b = c * part + n
                r = my_col * own + b
                total = cur_ref[b] + run_ref[plan_ref[3, r]] * plan_ref[4, r].astype(jnp.float32)
                for d in range(1, n_col):
                    level = code_in_ref[it, d, b].astype(jnp.int32).astype(jnp.float32) + 32768.0
                    total = total + level * (rows_in_ref[d, pl.ds(b, 1), :] * (1.0 / LEVELS))
                value = total * scale_ref[pl.ds(b, 1), :] + (1.0 - SPREAD) * prior_ref[:, lanes(b)]
                if it + 1 < ITERS:
                    cur_ref[b] = value
                    gathered[it + 1][my_row * own + b] = value.astype(jnp.bfloat16)
                else:
                    out_ref[:, lanes(b)] = value
                return carry

            lax.fori_loop(0, part, update, 0, unroll=True)
            if it + 1 < ITERS:
                sent += gather_start(it + 1, c)
        if it + 1 < ITERS:
            sent += gather_finish(it + 1)

    for copy in sent:
        copy.wait_send()


def local(n_row, n_col, labels_prior, tiles, tile_rows, tile_cols, tile_count):
    labels, piece = labels_prior.shape
    slots, tile, _ = tiles.shape
    own = piece // tile
    n_z = n_row // 2
    group = n_col * own
    smem = pl.BlockSpec(memory_space=pltpu.SMEM)
    width = -(-max(slots, group) // 128) * 128
    vmem = pl.BlockSpec(memory_space=pltpu.VMEM)
    return pl.pallas_call(
        functools.partial(kernel, n_row, n_col),
        out_shape=jax.ShapeDtypeStruct((labels, piece), jnp.float32),
        in_specs=[vmem, pl.BlockSpec(memory_space=pl.ANY), vmem, vmem, smem],
        out_specs=vmem,
        scratch_shapes=[
            pltpu.VMEM((slots, tile, tile), jnp.bfloat16),
            pltpu.VMEM((n_row * own, labels, tile), jnp.bfloat16),
            pltpu.VMEM((n_row * own, labels, tile), jnp.bfloat16),
            pltpu.VMEM((slots, labels, tile), jnp.float32),
            pltpu.VMEM((group, tile), jnp.float32),
            pltpu.VMEM((group, tile), jnp.float32),
            pltpu.VMEM((n_col, own, tile), jnp.float32),
            pltpu.VMEM((ITERS, group, labels, tile), jnp.int16),
            pltpu.VMEM((ITERS, n_col, own, labels, tile), jnp.int16),
            pltpu.VMEM((own, labels, tile), jnp.float32),
            pltpu.VMEM((own, tile), jnp.float32),
            pltpu.VMEM((8, width), jnp.int32),
            pltpu.SMEM((8, width), jnp.int32),
            pltpu.VMEM((slots, tile), jnp.float32),
            pltpu.SemaphoreType.DMA((LOADS,)),
            pltpu.SemaphoreType.DMA(()),
            pltpu.SemaphoreType.DMA((ITERS, 2 * n_z, CHUNKS)),
            pltpu.SemaphoreType.DMA((ITERS, 2 * n_z, CHUNKS)),
            pltpu.SemaphoreType.DMA((ITERS, n_col, CHUNKS)),
            pltpu.SemaphoreType.DMA((ITERS, n_col, CHUNKS)),
            pltpu.SemaphoreType.DMA((n_col,)),
            pltpu.SemaphoreType.DMA((n_col,)),
        ],
        compiler_params=pltpu.CompilerParams(
            collective_id=0, has_side_effects=True, vmem_limit_bytes=56 * 1024 * 1024
        ),
    )(labels_prior, tiles, tile_rows.reshape(1, -1), tile_cols.reshape(1, -1), tile_count)


def solution(mesh):
    n_row, n_col = mesh.shape["row"], mesh.shape["col"]
    in_specs = (
        P(None, ("row", "col")),
        P(("row", "col"), None, None),
        P(("row", "col")),
        P(("row", "col")),
        P(("row", "col")),
    )
    return jax.shard_map(
        functools.partial(local, n_row, n_col),
        mesh=mesh,
        in_specs=in_specs,
        out_specs=P(None, ("row", "col")),
        check_vma=False,
    )
```

```python
import functools

import jax
import jax.numpy as jnp
from jax import lax
from jax.experimental import pallas as pl
from jax.experimental.pallas import tpu as pltpu
from jax.sharding import PartitionSpec as P

ITERS = 2
SPREAD = 0.9
LEVELS = 65535.0
CHUNKS = 2
LOADS = 7
UNROLL = 56


def plan(rows, cols, count, table_ref, group_blocks):
    slots = rows.shape[1]
    lane = lax.broadcasted_iota(jnp.int32, (slots, slots), 1)
    down = lax.broadcasted_iota(jnp.int32, (slots, slots), 0)
    row = jnp.where(lane[0:1] < count, rows, group_blocks)
    key = row * slots + lane[0:1]
    same = lane == down

    def stand(x):
        return jnp.sum(jnp.where(same, x, 0), axis=1, keepdims=True)

    key_down, row_down, col_down = stand(key), stand(row), stand(cols)
    rank = jnp.sum((key < key_down).astype(jnp.int32), axis=1, keepdims=True)
    hit = rank == lane

    def lie(cond, x):
        return jnp.sum(jnp.where(cond, x, 0), axis=0, keepdims=True)

    here = lie(hit, row_down + 1)
    before = lie(rank + 1 == lane, row_down + 1)
    table_ref[0:1, 0:slots] = lie(hit, down)
    table_ref[1:2, 0:slots] = lie(hit, col_down)
    table_ref[2:3, 0:slots] = (here == before).astype(jnp.int32)
    group = lax.broadcasted_iota(jnp.int32, (slots, group_blocks), 1)
    stop = jnp.sum((row_down <= group).astype(jnp.int32), axis=0, keepdims=True)
    start = jnp.sum((row_down < group).astype(jnp.int32), axis=0, keepdims=True)
    table_ref[3:4, 0:group_blocks] = jnp.maximum(stop - 1, 0)
    table_ref[4:5, 0:group_blocks] = (stop > start).astype(jnp.int32)
    block = lax.broadcasted_iota(jnp.int32, (group_blocks, slots), 0)
    return (block == row).astype(jnp.float32)


def kernel(
    n_row, n_col,
    prior_hbm, tiles_hbm, slot_rows_ref, slot_cols_ref, count_ref,
    out_ref,
    prior_ref, tiles_ref, ag0_ref, ag1_ref, run_ref, rows_ref, inv_ref, rows_in_ref, code_ref, code_in_ref,
    cur_ref, scale_ref, table_ref, plan_ref, slot_sum_ref,
    prior_sem, load_sem, plan_sem, ag_send, ag_recv, rs_send, rs_recv, row_send, row_recv,
):
    labels, piece = prior_ref.shape
    slots, tile, _ = tiles_ref.shape
    own = piece // tile
    part = own // CHUNKS
    gathered = (ag0_ref, ag1_ref)
    n_z = n_row // 2
    my_row = lax.axis_index("row")
    my_col = lax.axis_index("col")
    my_z = my_row // 2
    my_core = my_row % 2
    partner = my_z * 2 + (1 - my_core)

    def at(row, col):
        return {"row": row, "col": col}

    prior_copy = pltpu.make_async_copy(prior_hbm, prior_ref, prior_sem)
    prior_copy.start()

    barrier = pltpu.get_barrier_semaphore()
    z_to = [None] + [((my_z + d) % n_z) * 2 + my_core for d in range(1, n_z)]
    z_from = [None] + [((my_z + n_z - d) % n_z) * 2 + my_core for d in range(1, n_z)]
    c_to = [None] + [(my_col + d) % n_col for d in range(1, n_col)]
    c_from = [None] + [(my_col + n_col - d) % n_col for d in range(1, n_col)]
    for d in range(1, n_z):
        pl.semaphore_signal(barrier, inc=1, device_id=at(z_to[d], my_col))
    pl.semaphore_signal(barrier, inc=1, device_id=at(partner, my_col))
    for d in range(1, n_col):
        pl.semaphore_signal(barrier, inc=1, device_id=at(my_row, c_to[d]))

    loads = []
    step = slots // LOADS
    for n in range(LOADS):
        window = pl.ds(n * step, step)
        loads.append(
            pltpu.make_async_copy(tiles_hbm.at[window], tiles_ref.at[window], load_sem.at[n])
        )
        loads[-1].start()

    def gather_copy(it, src_row, c, slot, to_row):
        window = pl.ds(src_row * own + c * part, part)
        return pltpu.make_async_remote_copy(
            src_ref=gathered[it].at[window],
            dst_ref=gathered[it].at[window],
            send_sem=ag_send.at[it, slot, c],
            recv_sem=ag_recv.at[it, slot, c],
            device_id=at(to_row, my_col),
        )

    def gather_start(it, c):
        copies = []
        for d in list(range(n_z - 1, 0, -1)):
            copies.append(gather_copy(it, my_row, c, d, z_to[d]))
        copies.append(gather_copy(it, my_row, c, n_z, partner))
        for copy in copies:
            copy.start()
        return copies

    def gather_finish(it):
        copies = []
        for c in range(CHUNKS):
            for d in range(1, n_z):
                gather_copy(it, z_from[d], c, d, z_to[d]).wait_recv()
                copy = gather_copy(it, z_from[d], c, n_z + d, partner)
                copy.start()
                copies.append(copy)
        for c in range(CHUNKS):
            for d in range(n_z):
                gather_copy(it, my_row, c, n_z + d, partner).wait_recv()
        return copies

    def lanes(b):
        return pl.ds(pl.multiple_of(b * tile, tile), tile)

    def round_prior(b, carry):
        value = prior_ref[:, lanes(b)]
        cur_ref[b] = value
        ag0_ref[my_row * own + b] = value.astype(jnp.bfloat16)
        return carry

    prior_copy.wait()
    lax.fori_loop(0, own, round_prior, 0, unroll=True)
    pl.semaphore_wait(barrier, n_z + n_col - 1)
    sent = []
    for c in range(CHUNKS):
        sent += gather_start(0, c)

    def product(left, right):
        return lax.dot_general(
            left, right, (((1,), (0,)), ((), ())), preferred_element_type=jnp.float32
        )

    hot = plan(slot_rows_ref[...], slot_cols_ref[...], count_ref[0], table_ref, n_col * own)
    plan_copy = pltpu.make_async_copy(table_ref, plan_ref, plan_sem)
    plan_copy.start()

    def pair(lefts, slot_pair):
        blank = jnp.zeros_like(lefts[0])
        left = jnp.concatenate(
            [
                jnp.concatenate([lefts[0], blank], axis=1),
                jnp.concatenate([blank, lefts[1]], axis=1),
            ],
            axis=0,
        )
        both = product(left, jnp.concatenate([tiles_ref[n] for n in slot_pair], axis=0))
        return both[:labels], both[labels:]

    ones = jnp.ones((labels, tile), jnp.bfloat16)
    for n, copy in enumerate(loads):
        copy.wait()

        def sum_pair(m, carry):
            k = n * step + 2 * m
            for turned in (k, k + 1):
                tiles_ref[turned] = tiles_ref[turned].T
            for i, value in enumerate(pair((ones, ones), (k, k + 1))):
                slot_sum_ref[pl.ds(k + i, 1), :] = value[0:1]
            return carry

        lax.fori_loop(0, step // 2, sum_pair, 0, unroll=True)
    rows_ref[...] = jnp.dot(
        hot, slot_sum_ref[...], precision=lax.Precision.HIGHEST, preferred_element_type=jnp.float32
    )

    def row_copy(d):
        return pltpu.make_async_remote_copy(
            src_ref=rows_ref.at[pl.ds(pl.multiple_of(c_to[d] * own, own), own)],
            dst_ref=rows_in_ref.at[d],
            send_sem=row_send.at[d],
            recv_sem=row_recv.at[d],
            device_id=at(my_row, c_to[d]),
        )

    for d in range(1, n_col):
        copy = row_copy(d)
        copy.start()
        sent.append(copy)
    whole = rows_ref[...]
    inv_ref[...] = jnp.where(whole > 0.0, LEVELS / jnp.where(whole > 0.0, whole, 1.0), 0.0)

    plan_copy.wait()
    sent += gather_finish(0)

    def code_copy(it, d, c):
        return pltpu.make_async_remote_copy(
            src_ref=code_ref.at[it, pl.ds(c_to[d] * own + c * part, part)],
            dst_ref=code_in_ref.at[it, d, pl.ds(c * part, part)],
            send_sem=rs_send.at[it, d, c],
            recv_sem=rs_recv.at[it, d, c],
            device_id=at(my_row, c_to[d]),
        )

    for it in range(ITERS):

        def add_pair(m, total):
            ks = (2 * m, 2 * m + 1)
            terms = pair(
                [gathered[it][plan_ref[1, k]] for k in ks], [plan_ref[0, k] for k in ks]
            )
            for k, term in zip(ks, terms):
                total = total * plan_ref[2, k].astype(jnp.float32) + term
                run_ref[k] = total
            return total

        lax.fori_loop(
            0, slots // 2, add_pair, jnp.zeros((labels, tile), jnp.float32), unroll=UNROLL
        )

        for c in range(CHUNKS):
            for d in range(1, n_col):

                def encode(b, carry):
                    r = c_to[d] * own + c * part + b
                    value = run_ref[plan_ref[3, r]] * plan_ref[4, r].astype(jnp.float32)
                    level = jnp.minimum(value * inv_ref[pl.ds(r, 1), :] + 0.5, LEVELS)
                    code_ref[it, r] = (level.astype(jnp.int32) - 32768).astype(jnp.int16)
                    return carry

                lax.fori_loop(0, part, encode, 0, unroll=True)
                copy = code_copy(it, d, c)
                copy.start()
                sent.append(copy)

        if it == 0:
            degree = 1.0 + rows_ref[pl.ds(pl.multiple_of(my_col * own, own), own), :]
            for d in range(1, n_col):
                row_copy(d).wait_recv()
                degree = degree + rows_in_ref[d]
            scale_ref[...] = SPREAD / degree

        for c in range(CHUNKS):
            for d in range(1, n_col):
                code_copy(it, d, c).wait_recv()

            def update(n, carry):
                b = c * part + n
                r = my_col * own + b
                total = cur_ref[b] + run_ref[plan_ref[3, r]] * plan_ref[4, r].astype(jnp.float32)
                for d in range(1, n_col):
                    level = code_in_ref[it, d, b].astype(jnp.int32).astype(jnp.float32) + 32768.0
                    total = total + level * (rows_in_ref[d, pl.ds(b, 1), :] * (1.0 / LEVELS))
                value = total * scale_ref[pl.ds(b, 1), :] + (1.0 - SPREAD) * prior_ref[:, lanes(b)]
                if it + 1 < ITERS:
                    cur_ref[b] = value
                    gathered[it + 1][my_row * own + b] = value.astype(jnp.bfloat16)
                else:
                    out_ref[:, lanes(b)] = value
                return carry

            lax.fori_loop(0, part, update, 0, unroll=True)
            if it + 1 < ITERS:
                sent += gather_start(it + 1, c)
        if it + 1 < ITERS:
            sent += gather_finish(it + 1)

    for copy in sent:
        copy.wait_send()


def local(n_row, n_col, labels_prior, tiles, tile_rows, tile_cols, tile_count):
    labels, piece = labels_prior.shape
    slots, tile, _ = tiles.shape
    own = piece // tile
    n_z = n_row // 2
    group = n_col * own
    smem = pl.BlockSpec(memory_space=pltpu.SMEM)
    width = -(-max(slots, group) // 128) * 128
    vmem = pl.BlockSpec(memory_space=pltpu.VMEM)
    return pl.pallas_call(
        functools.partial(kernel, n_row, n_col),
        out_shape=pltpu.VMEM((labels, piece), jnp.float32),
        in_specs=[pl.BlockSpec(memory_space=pl.ANY)] * 2 + [vmem, vmem, smem],
        out_specs=vmem,
        scratch_shapes=[
            pltpu.VMEM((labels, piece), jnp.float32),
            pltpu.VMEM((slots, tile, tile), jnp.bfloat16),
            pltpu.VMEM((n_row * own, labels, tile), jnp.bfloat16),
            pltpu.VMEM((n_row * own, labels, tile), jnp.bfloat16),
            pltpu.VMEM((slots, labels, tile), jnp.float32),
            pltpu.VMEM((group, tile), jnp.float32),
            pltpu.VMEM((group, tile), jnp.float32),
            pltpu.VMEM((n_col, own, tile), jnp.float32),
            pltpu.VMEM((ITERS, group, labels, tile), jnp.int16),
            pltpu.VMEM((ITERS, n_col, own, labels, tile), jnp.int16),
            pltpu.VMEM((own, labels, tile), jnp.float32),
            pltpu.VMEM((own, tile), jnp.float32),
            pltpu.VMEM((8, width), jnp.int32),
            pltpu.SMEM((8, width), jnp.int32),
            pltpu.VMEM((slots, tile), jnp.float32),
            pltpu.SemaphoreType.DMA(()),
            pltpu.SemaphoreType.DMA((LOADS,)),
            pltpu.SemaphoreType.DMA(()),
            pltpu.SemaphoreType.DMA((ITERS, 2 * n_z, CHUNKS)),
            pltpu.SemaphoreType.DMA((ITERS, 2 * n_z, CHUNKS)),
            pltpu.SemaphoreType.DMA((ITERS, n_col, CHUNKS)),
            pltpu.SemaphoreType.DMA((ITERS, n_col, CHUNKS)),
            pltpu.SemaphoreType.DMA((n_col,)),
            pltpu.SemaphoreType.DMA((n_col,)),
        ],
        compiler_params=pltpu.CompilerParams(
            collective_id=0, has_side_effects=True, vmem_limit_bytes=56 * 1024 * 1024
        ),
    )(labels_prior, tiles, tile_rows.reshape(1, -1), tile_cols.reshape(1, -1), tile_count)


def solution(mesh):
    n_row, n_col = mesh.shape["row"], mesh.shape["col"]
    in_specs = (
        P(None, ("row", "col")),
        P(("row", "col"), None, None),
        P(("row", "col")),
        P(("row", "col")),
        P(("row", "col")),
    )
    return jax.shard_map(
        functools.partial(local, n_row, n_col),
        mesh=mesh,
        in_specs=in_specs,
        out_specs=P(None, ("row", "col")),
        check_vma=False,
    )
```

```python
import functools

import jax
import jax.numpy as jnp
from jax import lax
from jax.experimental import pallas as pl
from jax.experimental.pallas import tpu as pltpu
from jax.sharding import PartitionSpec as P

ITERS = 2
SPREAD = 0.9
LEVELS = 65535.0
CHUNKS = 2
LOADS = 7
UNROLL = 56


def plan(rows, cols, count, table_ref, group_blocks):
    slots = rows.shape[1]
    lane = lax.broadcasted_iota(jnp.int32, (slots, slots), 1)
    down = lax.broadcasted_iota(jnp.int32, (slots, slots), 0)
    row = jnp.where(lane[0:1] < count, rows, group_blocks)
    key = row * slots + lane[0:1]
    same = lane == down

    def stand(x):
        return jnp.sum(jnp.where(same, x, 0), axis=1, keepdims=True)

    key_down, row_down, col_down = stand(key), stand(row), stand(cols)
    rank = jnp.sum((key < key_down).astype(jnp.int32), axis=1, keepdims=True)
    hit = rank == lane

    def lie(cond, x):
        return jnp.sum(jnp.where(cond, x, 0), axis=0, keepdims=True)

    here = lie(hit, row_down + 1)
    before = lie(rank + 1 == lane, row_down + 1)
    table_ref[0:1, 0:slots] = lie(hit, down)
    table_ref[1:2, 0:slots] = lie(hit, col_down)
    table_ref[2:3, 0:slots] = (here == before).astype(jnp.int32)
    group = lax.broadcasted_iota(jnp.int32, (slots, group_blocks), 1)
    stop = jnp.sum((row_down <= group).astype(jnp.int32), axis=0, keepdims=True)
    start = jnp.sum((row_down < group).astype(jnp.int32), axis=0, keepdims=True)
    table_ref[3:4, 0:group_blocks] = jnp.maximum(stop - 1, 0)
    table_ref[4:5, 0:group_blocks] = (stop > start).astype(jnp.int32)
    block = lax.broadcasted_iota(jnp.int32, (group_blocks, slots), 0)
    return (block == row).astype(jnp.float32)


def kernel(
    n_row, n_col,
    prior_hbm, tiles_hbm, slot_rows_ref, slot_cols_ref, count_ref,
    out_ref,
    prior_ref, tiles_ref, ag0_ref, ag1_ref, run_ref, rows_ref, inv_ref, rows_in_ref, code_ref, code_in_ref,
    cur_ref, scale_ref, table_ref, plan_ref, slot_sum_ref,
    prior_sem, load_sem, plan_sem, ag_send, ag_recv, rs_send, rs_recv, row_send, row_recv,
):
    labels, piece = prior_ref.shape
    slots, tile, _ = tiles_ref.shape
    own = piece // tile
    part = own // CHUNKS
    gathered = (ag0_ref, ag1_ref)
    n_z = n_row // 2
    my_row = lax.axis_index("row")
    my_col = lax.axis_index("col")
    my_z = my_row // 2
    my_core = my_row % 2
    partner = my_z * 2 + (1 - my_core)

    def at(row, col):
        return {"row": row, "col": col}

    prior_copy = pltpu.make_async_copy(prior_hbm, prior_ref, prior_sem)
    prior_copy.start()

    barrier = pltpu.get_barrier_semaphore()
    z_to = [None] + [((my_z + d) % n_z) * 2 + my_core for d in range(1, n_z)]
    z_from = [None] + [((my_z + n_z - d) % n_z) * 2 + my_core for d in range(1, n_z)]
    c_to = [None] + [(my_col + d) % n_col for d in range(1, n_col)]
    c_from = [None] + [(my_col + n_col - d) % n_col for d in range(1, n_col)]
    for d in range(1, n_z):
        pl.semaphore_signal(barrier, inc=1, device_id=at(z_to[d], my_col))
    pl.semaphore_signal(barrier, inc=1, device_id=at(partner, my_col))
    for d in range(1, n_col):
        pl.semaphore_signal(barrier, inc=1, device_id=at(my_row, c_to[d]))

    loads = []
    step = slots // LOADS
    for n in range(LOADS):
        window = pl.ds(n * step, step)
        loads.append(
            pltpu.make_async_copy(tiles_hbm.at[window], tiles_ref.at[window], load_sem.at[n])
        )
        loads[-1].start()

    def gather_copy(it, src_row, c, slot, to_row):
        window = pl.ds(src_row * own + c * part, part)
        return pltpu.make_async_remote_copy(
            src_ref=gathered[it].at[window],
            dst_ref=gathered[it].at[window],
            send_sem=ag_send.at[it, slot, c],
            recv_sem=ag_recv.at[it, slot, c],
            device_id=at(to_row, my_col),
        )

    def gather_start(it, c):
        copies = [gather_copy(it, my_row, c, n_z, partner)]
        for d in range(1, n_z):
            copies.append(gather_copy(it, my_row, c, d, z_to[d]))
        for copy in copies:
            copy.start()
        return copies

    def gather_finish(it):
        copies = []
        for c in range(CHUNKS):
            for d in range(1, n_z):
                gather_copy(it, z_from[d], c, d, z_to[d]).wait_recv()
                copy = gather_copy(it, z_from[d], c, n_z + d, partner)
                copy.start()
                copies.append(copy)
        for c in range(CHUNKS):
            for d in range(n_z):
                gather_copy(it, my_row, c, n_z + d, partner).wait_recv()
        return copies

    def lanes(b):
        return pl.ds(pl.multiple_of(b * tile, tile), tile)

    def round_prior(b, carry):
        value = prior_ref[:, lanes(b)]
        cur_ref[b] = value
        ag0_ref[my_row * own + b] = value.astype(jnp.bfloat16)
        return carry

    prior_copy.wait()
    lax.fori_loop(0, own, round_prior, 0, unroll=True)
    pl.semaphore_wait(barrier, n_z + n_col - 1)
    sent = []
    for c in range(CHUNKS):
        sent += gather_start(0, c)

    def product(left, right):
        return lax.dot_general(
            left, right, (((1,), (0,)), ((), ())), preferred_element_type=jnp.float32
        )

    hot = plan(slot_rows_ref[...], slot_cols_ref[...], count_ref[0], table_ref, n_col * own)
    plan_copy = pltpu.make_async_copy(table_ref, plan_ref, plan_sem)
    plan_copy.start()

    def pair(lefts, slot_pair):
        blank = jnp.zeros_like(lefts[0])
        left = jnp.concatenate(
            [
                jnp.concatenate([lefts[0], blank], axis=1),
                jnp.concatenate([blank, lefts[1]], axis=1),
            ],
            axis=0,
        )
        both = product(left, jnp.concatenate([tiles_ref[n] for n in slot_pair], axis=0))
        return both[:labels], both[labels:]

    ones = jnp.ones((labels, tile), jnp.bfloat16)
    for n, copy in enumerate(loads):
        copy.wait()

        def sum_pair(m, carry):
            k = n * step + 2 * m
            for turned in (k, k + 1):
                tiles_ref[turned] = tiles_ref[turned].T
            for i, value in enumerate(pair((ones, ones), (k, k + 1))):
                slot_sum_ref[pl.ds(k + i, 1), :] = value[0:1]
            return carry

        lax.fori_loop(0, step // 2, sum_pair, 0, unroll=True)
    rows_ref[...] = jnp.dot(
        hot, slot_sum_ref[...], precision=lax.Precision.HIGHEST, preferred_element_type=jnp.float32
    )

    def row_copy(d):
        return pltpu.make_async_remote_copy(
            src_ref=rows_ref.at[pl.ds(pl.multiple_of(c_to[d] * own, own), own)],
            dst_ref=rows_in_ref.at[d],
            send_sem=row_send.at[d],
            recv_sem=row_recv.at[d],
            device_id=at(my_row, c_to[d]),
        )

    for d in range(1, n_col):
        copy = row_copy(d)
        copy.start()
        sent.append(copy)
    whole = rows_ref[...]
    inv_ref[...] = jnp.where(whole > 0.0, LEVELS / jnp.where(whole > 0.0, whole, 1.0), 0.0)

    plan_copy.wait()
    sent += gather_finish(0)

    def code_copy(it, d, c):
        return pltpu.make_async_remote_copy(
            src_ref=code_ref.at[it, pl.ds(c_to[d] * own + c * part, part)],
            dst_ref=code_in_ref.at[it, d, pl.ds(c * part, part)],
            send_sem=rs_send.at[it, d, c],
            recv_sem=rs_recv.at[it, d, c],
            device_id=at(my_row, c_to[d]),
        )

    for it in range(ITERS):

        def add_pair(m, total):
            ks = (2 * m, 2 * m + 1)
            terms = pair(
                [gathered[it][plan_ref[1, k]] for k in ks], [plan_ref[0, k] for k in ks]
            )
            for k, term in zip(ks, terms):
                total = total * plan_ref[2, k].astype(jnp.float32) + term
                run_ref[k] = total
            return total

        lax.fori_loop(
            0, slots // 2, add_pair, jnp.zeros((labels, tile), jnp.float32), unroll=UNROLL
        )

        for c in range(CHUNKS):
            for d in range(1, n_col):

                def encode(b, carry):
                    r = c_to[d] * own + c * part + b
                    value = run_ref[plan_ref[3, r]] * plan_ref[4, r].astype(jnp.float32)
                    level = jnp.minimum(value * inv_ref[pl.ds(r, 1), :] + 0.5, LEVELS)
                    code_ref[it, r] = (level.astype(jnp.int32) - 32768).astype(jnp.int16)
                    return carry

                lax.fori_loop(0, part, encode, 0, unroll=True)
                copy = code_copy(it, d, c)
                copy.start()
                sent.append(copy)

        if it == 0:
            degree = 1.0 + rows_ref[pl.ds(pl.multiple_of(my_col * own, own), own), :]
            for d in range(1, n_col):
                row_copy(d).wait_recv()
                degree = degree + rows_in_ref[d]
            scale_ref[...] = SPREAD / degree

        for c in range(CHUNKS):
            for d in range(1, n_col):
                code_copy(it, d, c).wait_recv()

            def update(n, carry):
                b = c * part + n
                r = my_col * own + b
                total = cur_ref[b] + run_ref[plan_ref[3, r]] * plan_ref[4, r].astype(jnp.float32)
                for d in range(1, n_col):
                    level = code_in_ref[it, d, b].astype(jnp.int32).astype(jnp.float32) + 32768.0
                    total = total + level * (rows_in_ref[d, pl.ds(b, 1), :] * (1.0 / LEVELS))
                value = total * scale_ref[pl.ds(b, 1), :] + (1.0 - SPREAD) * prior_ref[:, lanes(b)]
                if it + 1 < ITERS:
                    cur_ref[b] = value
                    gathered[it + 1][my_row * own + b] = value.astype(jnp.bfloat16)
                else:
                    out_ref[:, lanes(b)] = value
                return carry

            lax.fori_loop(0, part, update, 0, unroll=True)
            if it + 1 < ITERS:
                sent += gather_start(it + 1, c)
        if it + 1 < ITERS:
            sent += gather_finish(it + 1)

    for copy in sent:
        copy.wait_send()


def local(n_row, n_col, labels_prior, tiles, tile_rows, tile_cols, tile_count):
    labels, piece = labels_prior.shape
    slots, tile, _ = tiles.shape
    own = piece // tile
    n_z = n_row // 2
    group = n_col * own
    smem = pl.BlockSpec(memory_space=pltpu.SMEM)
    width = -(-max(slots, group) // 128) * 128
    vmem = pl.BlockSpec(memory_space=pltpu.VMEM)
    return pl.pallas_call(
        functools.partial(kernel, n_row, n_col),
        out_shape=pltpu.VMEM((labels, piece), jnp.float32),
        in_specs=[pl.BlockSpec(memory_space=pl.ANY)] * 2 + [vmem, vmem, smem],
        out_specs=vmem,
        scratch_shapes=[
            pltpu.VMEM((labels, piece), jnp.float32),
            pltpu.VMEM((slots, tile, tile), jnp.bfloat16),
            pltpu.VMEM((n_row * own, labels, tile), jnp.bfloat16),
            pltpu.VMEM((n_row * own, labels, tile), jnp.bfloat16),
            pltpu.VMEM((slots, labels, tile), jnp.float32),
            pltpu.VMEM((group, tile), jnp.float32),
            pltpu.VMEM((group, tile), jnp.float32),
            pltpu.VMEM((n_col, own, tile), jnp.float32),
            pltpu.VMEM((ITERS, group, labels, tile), jnp.int16),
            pltpu.VMEM((ITERS, n_col, own, labels, tile), jnp.int16),
            pltpu.VMEM((own, labels, tile), jnp.float32),
            pltpu.VMEM((own, tile), jnp.float32),
            pltpu.VMEM((8, width), jnp.int32),
            pltpu.SMEM((8, width), jnp.int32),
            pltpu.VMEM((slots, tile), jnp.float32),
            pltpu.SemaphoreType.DMA(()),
            pltpu.SemaphoreType.DMA((LOADS,)),
            pltpu.SemaphoreType.DMA(()),
            pltpu.SemaphoreType.DMA((ITERS, 2 * n_z, CHUNKS)),
            pltpu.SemaphoreType.DMA((ITERS, 2 * n_z, CHUNKS)),
            pltpu.SemaphoreType.DMA((ITERS, n_col, CHUNKS)),
            pltpu.SemaphoreType.DMA((ITERS, n_col, CHUNKS)),
            pltpu.SemaphoreType.DMA((n_col,)),
            pltpu.SemaphoreType.DMA((n_col,)),
        ],
        compiler_params=pltpu.CompilerParams(
            collective_id=0, has_side_effects=True, vmem_limit_bytes=56 * 1024 * 1024
        ),
    )(labels_prior, tiles, tile_rows.reshape(1, -1), tile_cols.reshape(1, -1), tile_count)


def solution(mesh):
    n_row, n_col = mesh.shape["row"], mesh.shape["col"]
    in_specs = (
        P(None, ("row", "col")),
        P(("row", "col"), None, None),
        P(("row", "col")),
        P(("row", "col")),
        P(("row", "col")),
    )
    return jax.shard_map(
        functools.partial(local, n_row, n_col),
        mesh=mesh,
        in_specs=in_specs,
        out_specs=P(None, ("row", "col")),
        check_vma=False,
    )
```
